32 devices in a mesh: date: 16 (over z, y, core), tile: 2 (over x).
Axes of the slice: x: 2, y: 2, z: 4, core: 2. Of those that a mesh axis runs over, the one named last changes fastest.
Arguments:
- latest_model_output: float32 [2, 24, 16, 16, 64], P(None, None, None, 'tile', 'date'), may hold values from -6 to 6
- bygone_model_outputs: float32 [64, 24, 16, 16, 64], P('date', None, None, 'tile'), may hold values from -6 to 6
- sensor_reports: float32 [64, 24, 16, 64], P('date', None, 'tile'), may hold values from -6 to 6
- input_variable_scaling: float32 [16], replicated, may hold values from 0.25 to 4
- stepahead_blur_scale: float32 [24], replicated, may hold values from 0.02 to 0.08
- bygone_annual_ordinal: int32 [64], P('date'), may hold values from 0 to 364
- launch_annual_ordinal: int32 [2], replicated, may hold values from 0 to 364
Outputs:
- analog_mean: float32 [2, 24, 16, 64], P(None, None, 'tile', 'date')
The draws below stay inside these ranges and needn't reach their ends.
All inputs are finite; a program needn't handle non-finite values.
Results may differ from the reference program's by a relative error of at most 0.0003.
Values sent between devices are 32-bit elements; how exact they have to be, the bound alone decides.
No kernel may reach another device: no remote copies, remote signals or barrier semaphores. Data moves between devices by JAX's collectives and lax.ppermute only.
A program may use at most 128 MiB of HBM per device.

```python
import math
import jax
import jax.numpy as jnp
from jax import lax

INPUT_VARIABLES = 16
STEP_AHEAD_COUNT = 24
WIN_HALF = 3
CYCLES = 2
ARCHIVED_SAMPLES = 64
GRID_NORTHWARD = 16
GRID_EASTWARD = 64


def draw_latest_model_output(key, part):
    base_key = jax.random.fold_in(key, 11)
    extent = (CYCLES, STEP_AHEAD_COUNT, INPUT_VARIABLES, GRID_NORTHWARD, GRID_EASTWARD)
    values = jax.random.normal(base_key, extent, jnp.float32)
    return jnp.clip(values, -6.0, 6.0)


def expand_blocks(field):
    field = jnp.repeat(field, 8, axis=1)[:, :STEP_AHEAD_COUNT]
    field = jnp.repeat(field, 4, axis=3)[:, :, :, :GRID_NORTHWARD]
    field = jnp.repeat(field, 8, axis=4)[:, :, :, :, :GRID_EASTWARD]
    return field


def draw_bygone_model_outputs(key, part):
    extent = (ARCHIVED_SAMPLES, STEP_AHEAD_COUNT, INPUT_VARIABLES, GRID_NORTHWARD, GRID_EASTWARD)
    lead_blocks = (STEP_AHEAD_COUNT + 7) // 8
    row_blocks = (GRID_NORTHWARD + 3) // 4
    col_blocks = (GRID_EASTWARD + 7) // 8
    common = jax.random.uniform(jax.random.fold_in(key, 21), (1, lead_blocks, 1, row_blocks, col_blocks), jnp.float32, -3.0, 3.0)
    per_date = jax.random.uniform(jax.random.fold_in(key, 22), (ARCHIVED_SAMPLES, lead_blocks, 1, row_blocks, 1), jnp.float32, -1.0, 1.0)
    common_full = expand_blocks(common)
    per_date_full = expand_blocks(jnp.broadcast_to(per_date, (ARCHIVED_SAMPLES, lead_blocks, 1, row_blocks, col_blocks)))
    noise_key = jax.random.fold_in(key, 23)
    noise = jax.random.normal(noise_key, extent, jnp.float32)
    return jnp.clip(noise + common_full + per_date_full, -6.0, 6.0)


def with_ends(array, own_key, low, largest):
    dims = array.shape
    spot = [jax.random.randint(jax.random.fold_in(own_key, axis), (), 0, dims[axis]) for axis in range(len(dims))]
    array = array.at[tuple(spot)].set(low)
    longest = dims.index(max(dims))
    spot[longest] = (spot[longest] + 1) % dims[longest]
    return array.at[tuple(spot)].set(largest)


def level_of(own_key, shape, cuts, low, top_value):
    gain, own = 1.0, jax.random.fold_in(own_key, 6)
    for position, parts in cuts:
        heights = jnp.exp(jax.random.uniform(jax.random.fold_in(own, position), (parts,), jnp.float32, low / len(cuts), top_value / len(cuts)))
        gain = gain * jnp.repeat(heights, shape[position] // parts).reshape([-1 if axis == position else 1 for axis in range(len(shape))])
    return gain


def normal_values(rng, shape, scale, bound, pieces=(), held_as=jnp.bfloat16):
    drawn = scale * jax.random.normal(rng, shape, jnp.float32)
    if pieces:
        drawn = drawn * level_of(rng, shape, pieces, -0.22, 0.18)
    return jnp.clip(drawn, -bound, bound).astype(held_as)


def setup_inputs(seed: int = 0) -> dict:
    key_list = jax.random.split(jax.random.key(seed), 8)
    latest_model_output = draw_latest_model_output(jax.random.fold_in(key_list[7], 71), 0)
    bygone_model_outputs = draw_bygone_model_outputs(jax.random.fold_in(key_list[7], 71), 0)
    sensor_reports = normal_values(key_list[2], (ARCHIVED_SAMPLES, STEP_AHEAD_COUNT, GRID_NORTHWARD, GRID_EASTWARD), 1.0, 6.0, ((0, 16), (2, 2)), jnp.float32)
    input_variable_scaling = jnp.clip(jnp.exp(jax.random.uniform(key_list[3], (INPUT_VARIABLES,), jnp.float32, math.log(0.25), math.log(4.0))), 0.25, 4.0)
    stepahead_blur_scale = jnp.clip(jnp.exp(jax.random.uniform(key_list[4], (STEP_AHEAD_COUNT,), jnp.float32, math.log(0.02), math.log(0.08))), 0.02, 0.08)
    bygone_annual_ordinal = with_ends(jax.random.randint(key_list[5], (ARCHIVED_SAMPLES,), 0, 365), jax.random.fold_in(key_list[5], 1), 0, 364).astype(jnp.int32)
    launch_annual_ordinal = jax.random.randint(key_list[6], (CYCLES,), 0, 365).astype(jnp.int32)
    return {"latest_model_output": latest_model_output, "bygone_model_outputs": bygone_model_outputs, "sensor_reports": sensor_reports, "input_variable_scaling": input_variable_scaling, "stepahead_blur_scale": stepahead_blur_scale, "bygone_annual_ordinal": bygone_annual_ordinal, "launch_annual_ordinal": launch_annual_ordinal}


season_gain = 0.5


def window_sum(diffsq, reach):
    lead_count = diffsq.shape[-3]
    row_count = diffsq.shape[-2]
    col_count = diffsq.shape[-1]
    padded = jnp.pad(diffsq, [(0, 0)] * (diffsq.ndim - 3) + [(reach, reach), (1, 1), (1, 1)])
    totals = jnp.zeros(diffsq.shape, jnp.float32)
    for offset in range(2 * reach + 1):
        for row_off in range(3):
            for col_off in range(3):
                totals = totals + padded[..., offset:offset + lead_count, row_off:row_off + row_count, col_off:col_off + col_count]
    return totals / (9.0 * (2 * reach + 1))


def reference(latest_model_output, bygone_model_outputs, sensor_reports, input_variable_scaling, stepahead_blur_scale, bygone_annual_ordinal, launch_annual_ordinal):
    def single_sample(element):
        bygone_sample, calendar = element
        feature_discrepancy = latest_model_output - bygone_sample[None]
        diffsq = jnp.sum(feature_discrepancy * feature_discrepancy * input_variable_scaling[None, None, :, None, None], axis=2) / INPUT_VARIABLES
        season = season_gain * (1.0 - jnp.cos(2.0 * math.pi * (calendar - launch_annual_ordinal).astype(jnp.float32) / 365.0))
        return window_sum(diffsq, WIN_HALF) + season[:, None, None, None]

    analog_metric = lax.map(single_sample, (bygone_model_outputs, bygone_annual_ordinal))
    nearest = jnp.min(analog_metric, axis=0)
    spread_lead = stepahead_blur_scale[None, :, None, None]

    def accumulate(totals, element):
        distance, observed_day = element
        kernel = jnp.exp(-(distance - nearest) / spread_lead)
        return (totals[0] + kernel * observed_day[None], totals[1] + kernel), None

    zeros_field = jnp.zeros(nearest.shape, jnp.float32)
    (numer, denom), _ = lax.scan(accumulate, (zeros_field, zeros_field), (analog_metric, sensor_reports))
    return numer / denom
```

```python
import math

import jax
import jax.numpy as jnp
from jax import lax
from jax.experimental import pallas as pl
from jax.experimental.pallas import tpu as pltpu
from jax.sharding import PartitionSpec as P

WIN_HALF = 3
LANES = 128
season_gain = 0.5


def season_term(calendar, today):
    return season_gain * (
        1.0 - jnp.cos(2.0 * math.pi * (calendar - today).astype(jnp.float32) / 365.0)
    )


def swap(x, mask):
    size = lax.axis_size("date")
    return lax.ppermute(x, "date", [(i, i ^ mask) for i in range(size)])


def pack_forecast(latest):
    cycles, leads, variables, rows, cols = latest.shape
    points = cycles * variables * rows
    flat = jnp.transpose(latest, (0, 2, 3, 4, 1)).reshape(points * cols, leads)
    groups = points // LANES

    def kernel(in_ref, out_ref, wide_ref):
        wide_ref[:, 0:leads] = in_ref[...]
        for group in range(groups):
            for col in range(cols):
                start = group * LANES * cols + col
                part = wide_ref[pl.ds(start, LANES, stride=cols), :].T
                out_ref[group, col * leads : (col + 1) * leads, :] = part[0:leads]

    return pl.pallas_call(
        kernel,
        out_shape=jax.ShapeDtypeStruct((groups, cols * leads, LANES), jnp.float32),
        scratch_shapes=[pltpu.VMEM((points * cols, LANES), jnp.float32)],
        name="pack_forecast",
    )(flat)


def pack_archive(past, pack):
    dates, leads, variables, rows, cols = past.shape
    if pack == 1:
        return past
    step = 4 if leads % 4 == 0 else 1

    def kernel(*refs):
        refs[pack][...] = jnp.concatenate([ref[...] for ref in refs[:pack]], axis=-1)

    def spec(j):
        return pl.BlockSpec(
            (1, step, variables, rows, cols), lambda p, t: (p * pack + j, t, 0, 0, 0)
        )

    return pl.pallas_call(
        kernel,
        grid=(dates // pack, leads // step),
        in_specs=[spec(j) for j in range(pack)],
        out_specs=pl.BlockSpec(
            (1, step, variables, rows, pack * cols), lambda p, t: (p, t, 0, 0, 0)
        ),
        out_shape=jax.ShapeDtypeStruct(
            (dates // pack, leads, variables, rows, pack * cols), jnp.float32
        ),
        name="pack_archive",
    )(*[past] * pack)


def gather_forecast(own):
    size = lax.axis_size("date")
    blocks = {0: own}
    far = list(range(4, size, 4))
    for mask in far:
        blocks[mask] = swap(own, mask)
    blocks[2] = swap(own, 2)
    for mask in far:
        blocks[mask ^ 2] = swap(blocks[mask], 2)
    for mask in range(0, size, 2):
        blocks[mask ^ 1] = swap(blocks[mask], 1)
    return blocks


def shifted(x, axis, step):
    zero = jnp.zeros_like(lax.slice_in_dim(x, 0, abs(step), axis=axis))
    length = x.shape[axis]
    if step > 0:
        return jnp.concatenate([zero, lax.slice_in_dim(x, 0, length - step, axis=axis)], axis)
    return jnp.concatenate([lax.slice_in_dim(x, -step, length, axis=axis), zero], axis)


def window_kernel(masks, dims, place_ref, weight_ref, *refs):
    cycles, sets, leads, variables, rows, cols, block = dims
    pieces = refs[: len(masks)]
    past_ref, out_ref, edge_ref, field_ref, diff_ref, sem = refs[len(masks) :]
    copies = []
    for k, mask in enumerate(masks):
        start = pl.multiple_of((place_ref[0] ^ mask) * block, 8)
        copies.append(
            pltpu.make_async_copy(pieces[k], field_ref.at[:, pl.ds(start, block)], sem.at[k])
        )
    for copy in copies:
        copy.start()
    for copy in copies:
        copy.wait()
    groups = field_ref.shape[0]
    pack = LANES // cols
    per_group = LANES // rows

    def one_lead(lead, carry):
        fields = []
        for group in range(groups):
            now = field_ref[group, pl.ds(lead, cols, stride=leads), :]
            fields.append(jnp.concatenate([now] * pack, axis=0).T)
        for s in range(sets):
            totals = [None] * cycles
            for v in range(variables):
                past = past_ref[s, lead, v]
                for c in range(cycles):
                    k = c * variables + v
                    at = (k % per_group) * rows
                    gap = fields[k // per_group][at : at + rows] - past
                    term = gap * gap * weight_ref[v]
                    totals[c] = term if v == 0 else totals[c] + term
            for c in range(cycles):
                diff_ref[c * sets + s, lead] = totals[c]
        return carry

    lax.fori_loop(0, leads, one_lead, 0)
    lane = lax.broadcasted_iota(jnp.int32, (rows, LANES), 1) % cols
    zero = jnp.zeros((rows, LANES), jnp.float32)
    for k in range(cycles * sets):
        a = [diff_ref[k, t] for t in range(leads)]
        for t in range(leads):
            total = None
            for u in range(max(0, t - WIN_HALF), min(leads, t + WIN_HALF + 1)):
                total = a[u] if total is None else total + a[u]
            left = jnp.where(lane == 0, zero, pltpu.roll(total, 1, 1))
            right = jnp.where(lane == cols - 1, zero, pltpu.roll(total, LANES - 1, 1))
            at = (k * leads + t) * rows
            out_ref[at : at + rows, :] = total + left + right
    for k in range(cycles * sets):
        first = out_ref[pl.ds(k * leads * rows, leads, stride=rows), :]
        last = out_ref[pl.ds(k * leads * rows + rows - 1, leads, stride=rows), :]
        edge_ref[0, k * leads : (k + 1) * leads, :] = first
        edge_ref[1, k * leads : (k + 1) * leads, :] = last


def partial_kernel(dims, scale, place_ref, season_ref, spread_ref, sum_ref, above_ref, below_ref, report_ref, out_ref, rows_ref):
    cycles, sets, leads, rows, cols, own = dims
    pack = LANES // cols
    line = lax.broadcasted_iota(jnp.int32, (rows, LANES), 0)
    lane = lax.broadcasted_iota(jnp.int32, (rows, LANES), 1)
    at_first = jnp.logical_and(line == 0, place_ref[0] > 0)
    at_last = jnp.logical_and(line == rows - 1, place_ref[0] < place_ref[1] - 1)
    zero = jnp.zeros((rows, LANES), jnp.float32)
    seasons = []
    for k in range(cycles * sets):
        season = jnp.full((rows, LANES), season_ref[k * pack], jnp.float32)
        for j in range(1, pack):
            season = jnp.where(lane >= j * cols, season_ref[k * pack + j], season)
        seasons.append(season)

    def across(x, combine):
        total = x
        for j in range(1, pack):
            total = combine(total, pltpu.roll(x, j * cols, 1))
        return total

    def one(c, lead):
        gaps = []
        for s in range(sets):
            k = (c * sets + s) * leads + lead
            mid = sum_ref[pl.ds(pl.multiple_of(k * rows, 8), rows), :]
            above = above_ref[pl.ds(k, rows, stride=0), :]
            below = below_ref[pl.ds(k, rows, stride=0), :]
            up = jnp.where(line == 0, jnp.where(at_first, above, zero), pltpu.roll(mid, 1, 0))
            down = jnp.where(
                line == rows - 1, jnp.where(at_last, below, zero), pltpu.roll(mid, rows - 1, 0)
            )
            gaps.append((mid + up + down) * scale + seasons[c * sets + s])
        low = gaps[0]
        for gap in gaps[1:]:
            low = jnp.minimum(low, gap)
        low = across(low, jnp.minimum)
        spread = spread_ref[lead]
        numer = denom = None
        for s in range(sets):
            weight = jnp.exp((low - gaps[s]) / spread)
            report = [report_ref[s * pack + j, lead] for j in range(pack)]
            term = weight * (report[0] if pack == 1 else jnp.concatenate(report, axis=-1))
            numer = term if s == 0 else numer + term
            denom = weight if s == 0 else denom + weight
        numer, denom = across(numer, jnp.add), across(denom, jnp.add)
        start = c * rows * leads + lead
        rows_ref[0, pl.ds(start, rows, stride=leads), :] = numer / denom
        rows_ref[1, pl.ds(start, rows, stride=leads), :] = low - spread * jnp.log(denom)

    def body(lead, carry):
        for c in range(cycles):
            one(c, lead)
        return carry

    lax.fori_loop(0, leads, body, 0)
    for k in range(2):
        whole = rows_ref[k].T
        for source in range(cols // own):
            out_ref[source, k * own : (k + 1) * own, :] = whole[source * own : (source + 1) * own]


def merge_kernel(dims, spread_ref, part_ref, out_ref):
    size, own, leads, groups = dims
    low = part_ref[0, own : 2 * own, :]
    for k in range(1, size):
        low = jnp.minimum(low, part_ref[k, own : 2 * own, :])
    numer = denom = None
    for k in range(size):
        weight = jnp.exp((low - part_ref[k, own : 2 * own, :]) / spread_ref[...])
        term = weight * part_ref[k, 0:own, :]
        numer = term if k == 0 else numer + term
        denom = weight if k == 0 else denom + weight
    ratio = numer / denom
    for g in range(groups):
        out_ref[g] = ratio[:, g * leads : (g + 1) * leads]


def local(
    latest_model_output,
    bygone_model_outputs,
    sensor_reports,
    input_variable_scaling,
    stepahead_blur_scale,
    bygone_annual_ordinal,
    launch_annual_ordinal,
):
    cycles, leads, variables, rows, own = latest_model_output.shape
    dates, _, _, _, cols = bygone_model_outputs.shape
    size, tiles = lax.axis_size("date"), lax.axis_size("tile")
    smem = pl.BlockSpec(memory_space=pltpu.SMEM)
    vmem = pl.BlockSpec(memory_space=pltpu.VMEM)
    anywhere = pl.BlockSpec(memory_space=pl.ANY)
    pack = max(1, LANES // cols)
    sets = dates // pack
    block = own * leads
    count = cycles * sets * leads

    blocks = gather_forecast(pack_forecast(latest_model_output))
    masks = sorted(blocks)
    place = lax.axis_index("date").astype(jnp.int32).reshape(1)
    past = pack_archive(bygone_model_outputs, pack)
    dims = (cycles, sets, leads, variables, rows, cols, block)
    sums, edges = pl.pallas_call(
        lambda *refs: window_kernel(masks, dims, *refs),
        out_shape=(
            jax.ShapeDtypeStruct((count * rows, LANES), jnp.float32),
            jax.ShapeDtypeStruct((2, count, LANES), jnp.float32),
        ),
        in_specs=[smem, smem] + [anywhere] * len(masks) + [vmem],
        out_specs=(vmem, vmem),
        scratch_shapes=[
            pltpu.VMEM((cycles * variables * rows // LANES, cols * leads, LANES), jnp.float32),
            pltpu.VMEM((cycles * sets, leads, rows, LANES), jnp.float32),
            pltpu.SemaphoreType.DMA((len(masks),)),
        ],
        name="window_sums",
    )(place, input_variable_scaling, *[blocks[m] for m in masks], past)

    tile_place = lax.axis_index("tile").astype(jnp.int32)
    if tiles == 2:
        sent = jnp.where(tile_place == 0, edges[1], edges[0])
        above = below = lax.ppermute(sent, "tile", [(0, 1), (1, 0)])
    else:
        above = lax.ppermute(edges[1], "tile", [(i, i + 1) for i in range(tiles - 1)])
        below = lax.ppermute(edges[0], "tile", [(i + 1, i) for i in range(tiles - 1)])
    season = season_term(bygone_annual_ordinal[None, :], launch_annual_ordinal[:, None]).reshape(-1)
    scale = 1.0 / (variables * 9.0 * (2 * WIN_HALF + 1))
    points = cycles * rows * leads
    partial = pl.pallas_call(
        lambda *refs: partial_kernel((cycles, sets, leads, rows, cols, own), scale, *refs),
        out_shape=jax.ShapeDtypeStruct((size, 2 * own, points), jnp.float32),
        in_specs=[smem, smem, smem] + [vmem] * 4,
        out_specs=vmem,
        scratch_shapes=[pltpu.VMEM((2, points, LANES), jnp.float32)],
        name="partial_mean",
    )(
        jnp.stack([tile_place, jnp.int32(tiles)]),
        season,
        stepahead_blur_scale,
        sums,
        above,
        below,
        sensor_reports,
    )
    parts = lax.all_to_all(partial, "date", 0, 0)
    spread = jnp.tile(stepahead_blur_scale, cycles * rows)[None, :]
    groups = cycles * rows
    merged = pl.pallas_call(
        lambda *refs: merge_kernel((size, own, leads, groups), *refs),
        out_shape=jax.ShapeDtypeStruct((groups, own, leads), jnp.float32),
        in_specs=[vmem, vmem],
        out_specs=vmem,
        name="merge_parts",
    )(spread, parts)
    return jnp.transpose(merged.reshape(cycles, rows, own, leads), (0, 3, 1, 2))


def solution(mesh):
    placed = (
        P(None, None, None, "tile", "date"),
        P("date", None, None, "tile", None),
        P("date", None, "tile", None),
        P(),
        P(),
        P("date"),
        P(),
    )
    return jax.shard_map(
        local, mesh=mesh, in_specs=placed, out_specs=P(None, None, "tile", "date"), check_vma=False
    )
```

```python
import math

import jax
import jax.numpy as jnp
from jax import lax
from jax.experimental import pallas as pl
from jax.experimental.pallas import tpu as pltpu
from jax.sharding import PartitionSpec as P

WIN_HALF = 3
LANES = 128
KERNEL_PARAMS = pltpu.CompilerParams(vmem_limit_bytes=16 * 2**20)
season_gain = 0.5


def season_term(calendar, today):
    return season_gain * (
        1.0 - jnp.cos(2.0 * math.pi * (calendar - today).astype(jnp.float32) / 365.0)
    )


def swap(x, mask):
    size = lax.axis_size("date")
    return lax.ppermute(x, "date", [(i, i ^ mask) for i in range(size)])


def pack_forecast(latest):
    cycles, leads, variables, rows, cols = latest.shape
    points = cycles * variables * rows
    flat = jnp.transpose(latest, (0, 2, 3, 4, 1)).reshape(points * cols, leads)
    groups = points // LANES

    def kernel(in_ref, out_ref, wide_ref):
        wide_ref[:, 0:leads] = in_ref[...]
        for group in range(groups):
            for col in range(cols):
                start = group * LANES * cols + col
                part = wide_ref[pl.ds(start, LANES, stride=cols), :].T
                out_ref[group, col * leads : (col + 1) * leads, :] = part[0:leads]

    return pl.pallas_call(
        kernel,
        out_shape=jax.ShapeDtypeStruct((groups, cols * leads, LANES), jnp.float32),
        scratch_shapes=[pltpu.VMEM((points * cols, LANES), jnp.float32)],
        cost_estimate=pl.CostEstimate(flops=10**10, transcendentals=0, bytes_accessed=10**6),
        compiler_params=KERNEL_PARAMS,
        name="pack_forecast",
    )(flat)


def gather_forecast(own):
    size = lax.axis_size("date")
    blocks = {0: own}
    far = list(range(4, size, 4))
    for mask in far:
        blocks[mask] = swap(own, mask)
    blocks[2] = swap(own, 2)
    for mask in far:
        blocks[mask ^ 2] = swap(blocks[mask], 2)
    for mask in range(0, size, 2):
        blocks[mask ^ 1] = swap(blocks[mask], 1)
    return blocks


def shifted(x, axis, step):
    zero = jnp.zeros_like(lax.slice_in_dim(x, 0, abs(step), axis=axis))
    length = x.shape[axis]
    if step > 0:
        return jnp.concatenate([zero, lax.slice_in_dim(x, 0, length - step, axis=axis)], axis)
    return jnp.concatenate([lax.slice_in_dim(x, -step, length, axis=axis), zero], axis)


def window_kernel(masks, dims, weight_ref, *refs):
    cycles, sets, leads, variables, rows, cols, block = dims
    pieces = refs[: len(masks)]
    past_ref, out_ref = refs[len(masks) : len(masks) + 2]
    edge_refs = refs[len(masks) + 2 : -2]
    field_ref, diff_ref = refs[-2:]
    place = lax.axis_index("date")
    for k, mask in enumerate(masks):
        start = pl.multiple_of((place ^ mask) * block, 8)
        field_ref[:, pl.ds(start, block), :] = pieces[k][...]
    groups = field_ref.shape[0]
    pack = LANES // cols
    per_group = LANES // rows

    def one_lead(lead, carry):
        fields = []
        for group in range(groups):
            now = field_ref[group, pl.ds(lead, cols, stride=leads), :]
            fields.append(jnp.concatenate([now] * pack, axis=0).T)
        for s in range(sets):
            totals = [None] * cycles
            for v in range(variables):
                past = past_ref[s * pack, lead, v]
                if pack > 1:
                    more = [past_ref[s * pack + j, lead, v] for j in range(1, pack)]
                    past = jnp.concatenate([past] + more, axis=-1)
                for c in range(cycles):
                    k = c * variables + v
                    at = (k % per_group) * rows
                    gap = fields[k // per_group][at : at + rows] - past
                    term = gap * gap * weight_ref[v]
                    totals[c] = term if v == 0 else totals[c] + term
            for c in range(cycles):
                diff_ref[c * sets + s, lead] = totals[c]
        return carry

    lax.fori_loop(0, leads, one_lead, 0)
    lane = lax.broadcasted_iota(jnp.int32, (rows, LANES), 1) % cols
    zero = jnp.zeros((rows, LANES), jnp.float32)
    for k in range(cycles * sets):
        a = [diff_ref[k, t] for t in range(leads)]
        for t in range(leads):
            total = None
            for u in range(max(0, t - WIN_HALF), min(leads, t + WIN_HALF + 1)):
                total = a[u] if total is None else total + a[u]
            left = jnp.where(lane == 0, zero, pltpu.roll(total, 1, 1))
            right = jnp.where(lane == cols - 1, zero, pltpu.roll(total, LANES - 1, 1))
            at = (k * leads + t) * rows
            out_ref[at : at + rows, :] = total + left + right
    for k in range(cycles * sets):
        first = out_ref[pl.ds(k * leads * rows, leads, stride=rows), :]
        last = out_ref[pl.ds(k * leads * rows + rows - 1, leads, stride=rows), :]
        if len(edge_refs) == 1:
            edge_refs[0][k * leads : (k + 1) * leads, :] = jnp.where(
                lax.axis_index("tile") == 0, last, first
            )
        else:
            edge_refs[0][k * leads : (k + 1) * leads, :] = first
            edge_refs[1][k * leads : (k + 1) * leads, :] = last


def partial_kernel(dims, scale, season_ref, spread_ref, sum_ref, above_ref, below_ref, report_ref, out_ref, rows_ref):
    cycles, sets, leads, rows, cols, own = dims
    pack = LANES // cols
    line = lax.broadcasted_iota(jnp.int32, (rows, LANES), 0)
    lane = lax.broadcasted_iota(jnp.int32, (rows, LANES), 1)
    place, tiles = lax.axis_index("tile"), lax.axis_size("tile")
    at_first = jnp.logical_and(line == 0, place > 0)
    at_last = jnp.logical_and(line == rows - 1, place < tiles - 1)
    zero = jnp.zeros((rows, LANES), jnp.float32)
    seasons = []
    for k in range(cycles * sets):
        season = jnp.full((rows, LANES), season_ref[k * pack], jnp.float32)
        for j in range(1, pack):
            season = jnp.where(lane >= j * cols, season_ref[k * pack + j], season)
        seasons.append(season)

    def across(x, combine):
        total = x
        for j in range(1, pack):
            total = combine(total, pltpu.roll(x, j * cols, 1))
        return total

    def one(c, lead):
        gaps = []
        for s in range(sets):
            k = (c * sets + s) * leads + lead
            mid = sum_ref[pl.ds(pl.multiple_of(k * rows, 8), rows), :]
            above = above_ref[pl.ds(k, rows, stride=0), :]
            below = below_ref[pl.ds(k, rows, stride=0), :]
            up = jnp.where(line == 0, jnp.where(at_first, above, zero), pltpu.roll(mid, 1, 0))
            down = jnp.where(
                line == rows - 1, jnp.where(at_last, below, zero), pltpu.roll(mid, rows - 1, 0)
            )
            gaps.append((mid + up + down) * scale + seasons[c * sets + s])
        low = gaps[0]
        for gap in gaps[1:]:
            low = jnp.minimum(low, gap)
        low = across(low, jnp.minimum)
        spread = spread_ref[lead]
        numer = denom = None
        for s in range(sets):
            weight = jnp.exp((low - gaps[s]) / spread)
            report = [report_ref[s * pack + j, lead] for j in range(pack)]
            term = weight * (report[0] if pack == 1 else jnp.concatenate(report, axis=-1))
            numer = term if s == 0 else numer + term
            denom = weight if s == 0 else denom + weight
        numer, denom = across(numer, jnp.add), across(denom, jnp.add)
        start = c * rows * leads + lead
        rows_ref[0, pl.ds(start, rows, stride=leads), :] = numer / denom
        rows_ref[1, pl.ds(start, rows, stride=leads), :] = low - spread * jnp.log(denom)

    def body(lead, carry):
        for c in range(cycles):
            one(c, lead)
        return carry

    lax.fori_loop(0, leads, body, 0, unroll=4)
    for k in range(2):
        whole = rows_ref[k].T
        for source in range(cols // own):
            out_ref[source, k * own : (k + 1) * own, :] = whole[source * own : (source + 1) * own]


def merge_kernel(dims, spread_ref, part_ref, out_ref):
    size, own, leads, groups = dims
    low = part_ref[0, own : 2 * own, :]
    for k in range(1, size):
        low = jnp.minimum(low, part_ref[k, own : 2 * own, :])
    numer = denom = None
    for k in range(size):
        weight = jnp.exp((low - part_ref[k, own : 2 * own, :]) / spread_ref[...])
        term = weight * part_ref[k, 0:own, :]
        numer = term if k == 0 else numer + term
        denom = weight if k == 0 else denom + weight
    ratio = numer / denom
    for g in range(groups):
        out_ref[g] = ratio[:, g * leads : (g + 1) * leads]


def local(
    latest_model_output,
    bygone_model_outputs,
    sensor_reports,
    input_variable_scaling,
    stepahead_blur_scale,
    bygone_annual_ordinal,
    launch_annual_ordinal,
):
    cycles, leads, variables, rows, own = latest_model_output.shape
    dates, _, _, _, cols = bygone_model_outputs.shape
    size, tiles = lax.axis_size("date"), lax.axis_size("tile")
    smem = pl.BlockSpec(memory_space=pltpu.SMEM)
    vmem = pl.BlockSpec(memory_space=pltpu.VMEM)
    pack = max(1, LANES // cols)
    sets = dates // pack
    block = own * leads
    count = cycles * sets * leads

    blocks = gather_forecast(pack_forecast(latest_model_output))
    masks = sorted(blocks)
    dims = (cycles, sets, leads, variables, rows, cols, block)
    edge = jax.ShapeDtypeStruct((count, LANES), jnp.float32)
    edge_count = 1 if tiles == 2 else 2
    sums, *edges = pl.pallas_call(
        lambda *refs: window_kernel(masks, dims, *refs),
        out_shape=(
            jax.ShapeDtypeStruct((count * rows, LANES), jnp.float32),
            *[edge] * edge_count,
        ),
        in_specs=[smem] + [vmem] * len(masks) + [vmem],
        out_specs=(vmem,) * (1 + edge_count),
        scratch_shapes=[
            pltpu.VMEM((cycles * variables * rows // LANES, cols * leads, LANES), jnp.float32),
            pltpu.VMEM((cycles * sets, leads, rows, LANES), jnp.float32),
        ],
        compiler_params=KERNEL_PARAMS,
        name="window_sums",
    )(input_variable_scaling, *[blocks[m] for m in masks], bygone_model_outputs)

    if tiles == 2:
        above = below = lax.ppermute(edges[0], "tile", [(0, 1), (1, 0)])
    else:
        above = lax.ppermute(edges[1], "tile", [(i, i + 1) for i in range(tiles - 1)])
        below = lax.ppermute(edges[0], "tile", [(i + 1, i) for i in range(tiles - 1)])
    season = season_term(bygone_annual_ordinal[None, :], launch_annual_ordinal[:, None]).reshape(-1)
    scale = 1.0 / (variables * 9.0 * (2 * WIN_HALF + 1))
    points = cycles * rows * leads
    partial = pl.pallas_call(
        lambda *refs: partial_kernel((cycles, sets, leads, rows, cols, own), scale, *refs),
        out_shape=jax.ShapeDtypeStruct((size, 2 * own, points), jnp.float32),
        in_specs=[smem, smem] + [vmem] * 4,
        out_specs=vmem,
        scratch_shapes=[pltpu.VMEM((2, points, LANES), jnp.float32)],
        compiler_params=KERNEL_PARAMS,
        name="partial_mean",
    )(
        season,
        stepahead_blur_scale,
        sums,
        above,
        below,
        sensor_reports,
    )
    parts = lax.all_to_all(partial, "date", 0, 0)
    spread = jnp.tile(stepahead_blur_scale, cycles * rows)[None, :]
    groups = cycles * rows
    merged = pl.pallas_call(
        lambda *refs: merge_kernel((size, own, leads, groups), *refs),
        out_shape=jax.ShapeDtypeStruct((groups, own, leads), jnp.float32),
        in_specs=[vmem, vmem],
        out_specs=vmem,
        compiler_params=KERNEL_PARAMS,
        name="merge_parts",
    )(spread, parts)
    return jnp.transpose(merged.reshape(cycles, rows, own, leads), (0, 3, 1, 2))


def solution(mesh):
    placed = (
        P(None, None, None, "tile", "date"),
        P("date", None, None, "tile", None),
        P("date", None, "tile", None),
        P(),
        P(),
        P("date"),
        P(),
    )
    return jax.shard_map(
        local, mesh=mesh, in_specs=placed, out_specs=P(None, None, "tile", "date"), check_vma=False
    )
```
